128 devices in a mesh: dp: 128 (over z, x, y, core).
Axes of the slice: x: 4, y: 4, z: 4, core: 2. Of those that a mesh axis runs over, the one named last changes fastest.
Arguments:
- hidden: bfloat16 [256, 512, 2048], P('dp'), may hold values from -6 to 6
- lengths: int32 [256], P('dp'), may hold values from 1 to 512, 65536 in all
- order: int32 [256], P('dp'), may hold values from 0 to 255, each once
- candidates: int32 [256, 64], replicated, may hold values from 0 to 65535, as said below
- norm_gain: float32 [2048], replicated, may hold values from 0.25 to 1.75
- w_query: bfloat16 [2048, 1024], P('dp'), may hold values from -1 to 1
- w_key: bfloat16 [2048, 1024], P('dp'), may hold values from -1 to 1
- w_value: bfloat16 [2048, 1024], P('dp'), may hold values from -0.125 to 0.125
- w_out: bfloat16 [1024, 2048], P('dp'), may hold values from -0.75 to 0.75
- index_rows: bfloat16 [65536, 2048], P('dp'), may hold values from -0.125 to 0.125
Outputs:
- scores: float32 [256, 64], P('dp')
The draws below stay inside these ranges and needn't reach their ends.
Inputs may be any that keep to these rules, and one draw needn't show every extreme that they name: The candidates of many texts may all lie in the index rows of one device: in every draw at least half of the texts have all 64 of their candidates in the 512 index rows of one device, the same device for all of them.
All inputs are finite; a program needn't handle non-finite values. No bound on the sum of `lengths` on one device may be relied on, other than what follows from the above.
Results may differ from the reference program's by a relative error of at most 0.005.
Values may be sent and summed in bfloat16 or wider, within the bound.
No kernel may reach another device: no remote copies, remote signals or barrier semaphores. Data moves between devices by JAX's collectives and lax.ppermute only.
A program may use at most 128 MiB of HBM per device.

```python
import math
import jax
import jax.numpy as jnp
import numpy as np
from jax import lax

D = 2048
HEADS = 16
HEAD = 64
LMAX = 512
CAND = 64
ROWS_DEV = 512
HW = 1024
TEXTS = 256
ROWS = 65536


def weight_pair(key):
    base = jax.random.fold_in(key, 31)
    width = HEADS * HEAD
    key_part = jax.random.normal(jax.random.fold_in(base, 1), (D, width), jnp.float32) / math.sqrt(D)
    noise = jax.random.normal(jax.random.fold_in(base, 2), (D, width), jnp.float32) / math.sqrt(D * HEAD)
    query_part = noise
    return (jnp.clip(query_part, -1.0, 1.0), jnp.clip(key_part, -1.0, 1.0))


def draw_w_query(key, part):
    return weight_pair(key)[0].astype(jnp.bfloat16)


def draw_w_key(key, part):
    return weight_pair(key)[1].astype(jnp.bfloat16)


def draw_candidates(key, part):
    base = jax.random.fold_in(key, 57)
    shards = ROWS // ROWS_DEV
    chosen = jax.random.randint(jax.random.fold_in(base, 1), (), 0, shards, dtype=jnp.int32)
    ranking = jax.random.permutation(jax.random.fold_in(base, 2), jnp.arange(TEXTS, dtype=jnp.int32))
    nearby = chosen * ROWS_DEV + jax.random.randint(jax.random.fold_in(base, 3), (TEXTS, CAND), 0, ROWS_DEV, dtype=jnp.int32)
    first = jax.random.randint(jax.random.fold_in(base, 4), (TEXTS, CAND), 0, ROWS, dtype=jnp.int32)
    second = jax.random.randint(jax.random.fold_in(base, 5), (TEXTS, CAND), 0, ROWS, dtype=jnp.int32)
    relabel = jax.random.permutation(jax.random.fold_in(base, 6), jnp.arange(ROWS, dtype=jnp.int32))
    spread_rows = relabel[jnp.minimum(first, second)]
    result = jnp.where((ranking < TEXTS // 2)[:, None], nearby, spread_rows)
    coldest = jnp.argmax(ranking).astype(jnp.int32)
    result = result.at[coldest, 0].set(0).at[coldest, 1].set(ROWS - 1)
    return result.astype(jnp.int32)


def levels(rng, extent, pieces, least, high):
    gain = 1.0
    for dim, blocks in pieces:
        heights = jax.random.uniform(jax.random.fold_in(jax.random.fold_in(rng, 6), dim), (blocks,), jnp.float32, least / len(pieces), high / len(pieces))
        gain = gain * jnp.repeat(jnp.exp(heights), extent[dim] // blocks).reshape((-1,) + (1,) * (len(extent) - 1 - dim))
    return gain


def split_up(count, total, most, slope):
    portions = [(1 << 20) // math.isqrt(standing ** slope) + 1 for standing in range(2, count + 1)]
    rest, holding = total - most - (count - 1), [1] * (count - 1)
    while rest > 0:
        free = [i for i in range(count - 1) if holding[i] < most]
        mass, left = sum([portions[i] for i in free]), rest
        for i in free:
            addition = min(most - holding[i], max(1, left * portions[i] // mass), rest)
            holding[i] = holding[i] + addition
            rest = rest - addition
    return np.array([most] + holding)


def ragged_sizes(own_key, count, total, bound, slope):
    if count == 2:
        one = jax.random.randint(own_key, (), max(1, total - bound), min(bound, total - 1) + 1)
        return jnp.stack([one, total - one])
    sizes = jnp.asarray(split_up(count, total, bound, slope), jnp.int32)
    pairs = (count - 1) // 2
    giver, receiver = sizes[1:1 + 2 * pairs:2], sizes[2:2 + 2 * pairs:2]
    slack = jnp.minimum(giver - 1, bound - receiver)
    moved = jax.random.randint(jax.random.fold_in(own_key, 1), (pairs,), 0, 1 << 20) % (slack + 1)
    sizes = sizes.at[1:1 + 2 * pairs:2].set(giver - moved).at[2:2 + 2 * pairs:2].set(receiver + moved)
    return sizes[jax.random.permutation(jax.random.fold_in(own_key, 2), count)]


def gaussian(own_key, extent, scale, bound, cuts=(), held_as=jnp.bfloat16):
    values = scale * jax.random.normal(own_key, extent, jnp.float32)
    if cuts:
        values = values * levels(own_key, extent, cuts, -0.22, 0.18)
    return jnp.clip(values, -bound, bound).astype(held_as)


def setup_inputs(seed: int = 0) -> dict:
    seeds = jax.random.split(jax.random.key(seed), 11)
    return {
        "hidden": gaussian(seeds[0], (TEXTS, LMAX, D), 1.0, 6.0, ((0, 128),)),
        "lengths": ragged_sizes(seeds[1], TEXTS, TEXTS * LMAX // 2, LMAX, 2).astype(jnp.int32),
        "order": jax.random.permutation(seeds[2], TEXTS).astype(jnp.int32),
        "candidates": draw_candidates(jax.random.fold_in(seeds[10], 71), 0),
        "norm_gain": jnp.clip(1.0 + 0.15 * jax.random.normal(seeds[4], (D,), jnp.float32), 0.25, 1.75),
        "w_query": draw_w_query(jax.random.fold_in(seeds[10], 71), 0),
        "w_key": draw_w_key(jax.random.fold_in(seeds[10], 71), 0),
        "w_value": gaussian(seeds[7], (D, HW), D ** -0.5, 0.125, ((0, 128),)),
        "w_out": gaussian(seeds[8], (HW, D), HEAD ** -0.5, 0.75, ((0, 128),)),
        "index_rows": gaussian(seeds[9], (ROWS, D), D ** -0.5, 0.125, ((0, 128),)),
    }


def encode_text(text, length, norm_gain, w_query, w_key, w_value, w_out):
    values_f = text.astype(jnp.float32)
    meansq = lax.optimization_barrier(jnp.mean(values_f * values_f, axis=-1, keepdims=True))
    normed = (values_f * lax.rsqrt(meansq + 1e-06) * norm_gain).astype(jnp.bfloat16)
    queries = jnp.dot(normed, w_query, preferred_element_type=jnp.float32).astype(jnp.bfloat16)
    key_side = jnp.dot(normed, w_key, preferred_element_type=jnp.float32).astype(jnp.bfloat16)
    value_side = jnp.dot(normed, w_value, preferred_element_type=jnp.float32).astype(jnp.bfloat16)
    queries = queries.reshape(LMAX, HEADS, HEAD).astype(jnp.float32)
    key_side = key_side.reshape(LMAX, HEADS, HEAD).astype(jnp.float32)
    value_side = value_side.reshape(LMAX, HEADS, HEAD).astype(jnp.float32)
    logits = jnp.einsum('qhd,khd->hqk', queries, key_side)
    valid = jnp.arange(LMAX, dtype=jnp.int32) < length
    logits = jnp.where(valid[None, None, :], logits, jnp.float32(-1e+30))
    probs = jax.nn.softmax(logits, axis=-1).astype(jnp.bfloat16)
    context = jnp.einsum('hqk,khd->qhd', probs.astype(jnp.float32), value_side)
    context = context.astype(jnp.bfloat16).reshape(LMAX, HEADS * HEAD)
    layer_out = values_f + jnp.dot(context, w_out, preferred_element_type=jnp.float32)
    pooled = lax.optimization_barrier(jnp.sum(jnp.where(valid[:, None], layer_out, jnp.float32(0.0)), axis=0)) / length.astype(jnp.float32)
    unit = pooled * lax.rsqrt(jnp.mean(pooled * pooled) + 1e-06)
    return unit.astype(jnp.bfloat16)

def reference(hidden, lengths, order, candidates, norm_gain, w_query, w_key, w_value, w_out, index_rows):

    def one_text(pair):
        return encode_text(pair[0], pair[1], norm_gain, w_query, w_key, w_value, w_out)
    units = lax.map(one_text, (hidden, lengths))
    cand_proc = candidates[order]

    def score_text(pair):
        rows = index_rows[pair[1]].astype(jnp.float32)
        return jnp.dot(rows, pair[0].astype(jnp.float32), precision=lax.Precision.HIGHEST)
    scores_proc = lax.map(score_text, (units, cand_proc))
    scores = jnp.zeros((TEXTS, CAND), jnp.float32).at[order].set(scores_proc)
    return scores
```

```python
import functools

import jax
import jax.numpy as jnp
from jax import lax
from jax.experimental import pallas as pl
from jax.experimental.pallas import tpu as pltpu
from jax.sharding import PartitionSpec as P

HEAD = 64
NEG = -1e30
bf16 = jnp.bfloat16
f32 = jnp.float32


def split(x):
    hi = x.astype(bf16)
    return hi, (x - hi.astype(f32)).astype(bf16)


def attend_kernel(lens_ref, n_ref, w_ref, g_ref, qk_ref, col_ref, *, heads):
    slots = n_ref.shape[1]
    length = lens_ref[pl.program_id(0)]
    blocks = (length + 127) // 128
    pairs = heads // 2

    def run(size):
        rows = n_ref[0, :size, :]
        for tile in range(heads // 2):
            out = jnp.dot(
                rows, w_ref[:, tile * 256 : (tile + 1) * 256], preferred_element_type=f32
            ).astype(bf16)
            qk_ref[2 * tile, :size, :] = out[:, :128]
            qk_ref[2 * tile + 1, :size, :] = out[:, 128:]
        col_ref[...] = jnp.zeros_like(col_ref)
        tail = size - 128
        key_id = tail + lax.broadcasted_iota(jnp.int32, (128, 1), 0)

        def pair(p, carry):
            keys = qk_ref[pairs + p, :size, :]
            lane = lax.broadcasted_iota(jnp.int32, (size, 128), 1)
            for half in range(2):
                key_half = jnp.where((lane < HEAD) == (half == 0), keys, jnp.zeros_like(keys))
                acc = jnp.zeros((size, 128), f32)
                for start in range(0, size, 128):
                    query = qk_ref[p, start : start + 128, :]
                    s = lax.dot_general(
                        key_half, query, (((1,), (1,)), ((), ())), preferred_element_type=f32
                    )
                    last = jnp.where(key_id < length, s[tail:, :], NEG)
                    s = jnp.concatenate([s[:tail, :], last], axis=0) if tail else last
                    e = jnp.exp(s - jnp.max(s, axis=0, keepdims=True))
                    total = jnp.sum(e, axis=0, keepdims=True)
                    query_id = start + lax.broadcasted_iota(jnp.int32, (1, 128), 1)
                    acc = acc + e * jnp.where(query_id < length, 1.0 / total, 0.0)
                column = jnp.sum(acc, axis=1, keepdims=True)
                col_ref[:size, :] = jnp.where(lane == 2 * p + half, column, col_ref[:size, :])
            return carry

        lax.fori_loop(0, pairs, pair, 0)
        hi, lo = split(col_ref[:size, :])
        dims = (((0,), (0,)), ((), ()))
        g = lax.dot_general(hi, rows, dims, preferred_element_type=f32)
        g = g + lax.dot_general(lo, rows, dims, preferred_element_type=f32)
        g_ref[0] = g[:heads, :]

    for b in range(1, slots // 128 + 1):
        pl.when(blocks == b)(functools.partial(run, 128 * b))


def attend(lens, normed, weights, heads):
    texts, slots, width = normed.shape
    cols = 2 * heads * HEAD
    return pl.pallas_call(
        functools.partial(attend_kernel, heads=heads),
        grid_spec=pltpu.PrefetchScalarGridSpec(
            num_scalar_prefetch=1,
            grid=(texts,),
            in_specs=[
                pl.BlockSpec((1, slots, width), lambda t, n: (t, 0, 0)),
                pl.BlockSpec((width, cols), lambda t, n: (0, 0), pipeline_mode=pl.Buffered(1)),
            ],
            out_specs=pl.BlockSpec((1, heads, width), lambda t, n: (t, 0, 0)),
            scratch_shapes=[
                pltpu.VMEM((heads, slots, 128), bf16),
                pltpu.VMEM((slots, 128), f32),
            ],
        ),
        out_shape=jax.ShapeDtypeStruct((texts, heads, width), f32),
        compiler_params=pltpu.CompilerParams(vmem_limit_bytes=48 << 20),
        cost_estimate=pl.CostEstimate(
            flops=2 * texts * slots * width * cols,
            bytes_accessed=2 * (texts * slots * width + width * cols),
            transcendentals=texts * heads * slots * slots,
        ),
        name="attend",
    )(lens, normed, weights)


def context_kernel(g_ref, w_ref, out_ref, *, texts, heads):
    g = g_ref[...].reshape(texts * heads, g_ref.shape[2])
    hi, lo = split(g)
    both = jnp.dot(jnp.concatenate([hi, lo], axis=0), w_ref[...], preferred_element_type=f32)
    both = (both[: texts * heads] + both[texts * heads :]).reshape(texts, heads, heads * HEAD)
    head = lax.broadcasted_iota(jnp.int32, both.shape, 1)
    lane = lax.broadcasted_iota(jnp.int32, both.shape, 2)
    own = jnp.sum(jnp.where(lane // HEAD == head, both, 0.0), axis=1)
    out_ref[...] = jnp.concatenate([own, jnp.zeros_like(own)], axis=0)


def context_of(g, w_value):
    texts, heads, width = g.shape
    return pl.pallas_call(
        functools.partial(context_kernel, texts=texts, heads=heads),
        grid=(1,),
        in_specs=[
            pl.BlockSpec((texts, heads, width), lambda i: (0, 0, 0)),
            pl.BlockSpec((width, heads * HEAD), lambda i: (0, 0)),
        ],
        out_specs=pl.BlockSpec((2 * texts, heads * HEAD), lambda i: (0, 0)),
        out_shape=jax.ShapeDtypeStruct((2 * texts, heads * HEAD), f32),
        name="context",
    )(g, w_value)


def unit_kernel(core_ref, mine_ref, theirs_ref, wa_ref, wb_ref, sum_ref, len_ref, ord_ref, out_ref):
    core = core_ref[0]
    half = mine_ref.shape[1]
    width = sum_ref.shape[1]
    cols = wa_ref.shape[1]
    mine = jnp.concatenate(split(mine_ref[...]), axis=0)
    theirs = jnp.concatenate(split(theirs_ref[...]), axis=0)
    rows = mine_ref.shape[0]

    def project(w_ref):
        top = w_ref[pl.ds(pl.multiple_of(core * half, half), half), :]
        bottom = w_ref[pl.ds(pl.multiple_of((1 - core) * half, half), half), :]
        a = jnp.dot(mine, top, preferred_element_type=f32)
        b = jnp.dot(theirs, bottom, preferred_element_type=f32)
        return (a[0:2] + a[rows : rows + 2]) + (b[2:4] + b[rows + 2 : rows + 4])

    near = pl.ds(pl.multiple_of(core * cols, cols), cols)
    far = pl.ds(pl.multiple_of((1 - core) * cols, cols), cols)
    inv = 1.0 / len_ref[...]
    pa = (sum_ref[:, near] + project(wa_ref)) * inv
    pb = (sum_ref[:, far] + project(wb_ref)) * inv
    square = jnp.sum(pa * pa, axis=1, keepdims=True) + jnp.sum(pb * pb, axis=1, keepdims=True)
    scale = lax.rsqrt(square * (1.0 / width) + 1e-06)
    out_ref[:, near] = (pa * scale).astype(bf16)
    out_ref[:, far] = (pb * scale).astype(bf16)
    out_ref[:, width:] = jnp.broadcast_to(ord_ref[...], (2, 128)).astype(bf16)


def unit_of(core, mine, theirs, wa, wb, total, lens, order):
    texts, width = total.shape
    vmem = pl.BlockSpec(memory_space=pltpu.VMEM)
    return pl.pallas_call(
        unit_kernel,
        in_specs=[pl.BlockSpec(memory_space=pltpu.SMEM)] + [vmem] * 7,
        out_specs=vmem,
        out_shape=jax.ShapeDtypeStruct((texts, width + 128), bf16),
        name="unit",
    )(core, mine, theirs, wa, wb, total, lens, order)


def score_kernel(dev_ref, ua_ref, ub_ref, rows_ref, cand_ref, out_ref):
    own, width = rows_ref.shape
    pairs = cand_ref.shape[0]
    near = cand_ref[...] - dev_ref[0] * own
    valid = (near >= 0) & (near < own)
    tile = near // 128
    within = jnp.where(valid, near - tile * 128, 0)
    lane = lax.broadcasted_iota(jnp.int32, near.shape, 1)
    picked = jnp.zeros(near.shape, f32)
    for odd in range(2):
        units = jnp.zeros((pairs, width), f32)
        for u_ref in (ua_ref, ub_ref):
            rank = u_ref[:, width:].astype(f32)
            place = 2 * lax.broadcasted_iota(jnp.int32, rank.shape, 1) + odd
            hot = (rank == place.astype(f32)).astype(bf16)
            units = units + lax.dot_general(
                hot, u_ref[:, :width], (((0,), (0,)), ((), ())), preferred_element_type=f32
            )
        local = lax.dot_general(
            units.astype(bf16), rows_ref[...], (((1,), (1,)), ((), ())), preferred_element_type=f32
        )
        side = valid & ((lane >= 64) == (odd == 1))
        for k in range(own // 128):
            got = jnp.take_along_axis(local[:, k * 128 : (k + 1) * 128], within, axis=1)
            picked = jnp.where(side & (tile == k), got, picked)
    out_ref[...] = picked


def scores_of(device, ua, ub, rows, cand):
    vmem = pl.BlockSpec(memory_space=pltpu.VMEM)
    return pl.pallas_call(
        score_kernel,
        in_specs=[pl.BlockSpec(memory_space=pltpu.SMEM)] + [vmem] * 4,
        out_specs=vmem,
        out_shape=jax.ShapeDtypeStruct(cand.shape, f32),
        compiler_params=pltpu.CompilerParams(vmem_limit_bytes=32 << 20),
        name="scores",
    )(device, ua, ub, rows, cand)


def per_device(
    devices, hidden, lengths, order, candidates, norm_gain, w_query, w_key, w_value, w_out, index_rows
):
    texts, slots, width = hidden.shape
    features = w_query.shape[1]
    half = features // 2
    heads = half // HEAD
    device = lax.axis_index("dp")
    core = device % 2
    swap_pairs = [(d, d ^ 1) for d in range(devices)]
    same_core = [list(range(c, devices, 2)) for c in range(2)]

    def swap(x):
        return lax.ppermute(x, "dp", swap_pairs)

    def share(w):
        cols = w.shape[1] // 2
        keep = lax.dynamic_slice_in_dim(w, core * cols, cols, 1)
        give = lax.dynamic_slice_in_dim(w, (1 - core) * cols, cols, 1)
        got = swap(give)
        first = jnp.where(core == 0, keep, got)
        second = jnp.where(core == 0, got, keep)
        return jnp.concatenate([first, second], axis=0)

    block = jnp.concatenate(
        [share(w_query), share(w_key), share(w_value), share(w_out).reshape(32, half)], axis=1
    )
    weights = lax.all_gather(block, "dp", axis=0, tiled=True, axis_index_groups=same_core)

    values = hidden.astype(f32)
    meansq = jnp.mean(values * values, axis=-1, keepdims=True)
    normed = (values * lax.rsqrt(meansq + 1e-06) * norm_gain).astype(bf16)
    normed = jnp.concatenate([normed, swap(normed)], axis=0)
    lens = jnp.concatenate([lengths, swap(lengths)])
    valid = jnp.arange(slots, dtype=jnp.int32)[None, :] < lengths[:, None]
    total = jnp.sum(jnp.where(valid[:, :, None], values, 0.0), axis=1)

    g = attend(lens, normed, weights, heads)
    mine = context_of(g, weights[:, 2 * half : 3 * half])
    wo_near = weights[:, 3 * half :].reshape(features, width // 2)
    wo_far = swap(wo_near)
    theirs = swap(mine)
    unit = unit_of(
        core.reshape(1),
        mine,
        theirs,
        wo_near,
        wo_far,
        total,
        lengths.astype(f32).reshape(texts, 1),
        order.astype(f32).reshape(texts, 1),
    )
    copies = jnp.broadcast_to(unit[None], (devices // 2,) + unit.shape)
    units = lax.all_to_all(copies, "dp", 0, 0, tiled=True, axis_index_groups=same_core)
    ua = units.reshape(devices, unit.shape[1])
    ub = swap(ua)
    cand = candidates.reshape(devices, 2 * candidates.shape[1])
    picked = scores_of(device.reshape(1), ua, ub, index_rows, cand)
    back = lax.all_to_all(picked.reshape(devices, 1, picked.shape[1]), "dp", 0, 0, tiled=True)
    return jnp.sum(back, axis=(0, 1)).reshape(texts, candidates.shape[1])


def solution(mesh):
    devices = mesh.shape["dp"]
    return jax.shard_map(
        functools.partial(per_device, devices),
        mesh=mesh,
        in_specs=(
            P("dp", None, None),
            P("dp"),
            P("dp"),
            P(),
            P(),
            P("dp", None),
            P("dp", None),
            P("dp", None),
            P("dp", None),
            P("dp", None),
        ),
        out_specs=P("dp", None),
        check_vma=False,
    )
```

```python
import functools

import jax
import jax.numpy as jnp
from jax import lax
from jax.experimental import pallas as pl
from jax.experimental.pallas import tpu as pltpu
from jax.sharding import PartitionSpec as P

HEAD = 64
SIDE = 4
GROUPS = 2
NEG = -1e30
bf16 = jnp.bfloat16
f32 = jnp.float32


def split(x):
    hi = x.astype(bf16)
    return hi, (x - hi.astype(f32)).astype(bf16)

ANY = pl.BlockSpec(memory_space=pl.ANY)
VMEM = pl.BlockSpec(memory_space=pltpu.VMEM)
SMEM = pl.BlockSpec(memory_space=pltpu.SMEM)


def position(device):
    return device // 32, (device // 8) % SIDE, (device // 2) % SIDE, device % 2


def wrap(i):
    return lax.rem(i, SIDE)


def block_kernel(dev_ref, q, k, v, o, pq, pk, pv, po, qk_ref, vo_ref):
    core = position(dev_ref[0])[3]

    def both(own, other, start, cols):
        at = pl.ds(pl.multiple_of(core * (own.shape[1] // 2) + start, cols), cols)
        a, b = own[:, at], other[:, at]
        return jnp.concatenate([jnp.where(core == 0, a, b), jnp.where(core == 0, b, a)], axis=0)

    half = q.shape[1] // 2
    qk_ref[:, :half] = both(q, pq, 0, half)
    qk_ref[:, half:] = both(k, pk, 0, half)
    vo_ref[:, :half] = both(v, pv, 0, half)
    rows = 2 * o.shape[0]
    vo_ref[:rows, half:] = both(o, po, 0, half)
    vo_ref[rows:, half:] = both(o, po, half, half)


def first_qk_kernel(dev_ref, *refs):
    y = position(dev_ref[0])[2]
    q_ref, k_ref = refs[SIDE:]
    half = q_ref.shape[2]
    for i in range(SIDE):
        q_ref[wrap(y + i)] = refs[i][:, :half]
        k_ref[wrap(y + i)] = refs[i][:, half:]


def first_vo_kernel(dev_ref, *refs):
    x = position(dev_ref[0])[1]
    for i in range(SIDE):
        refs[SIDE][wrap(x + i)] = refs[i][...]


def second_qk_kernel(dev_ref, *refs):
    z, x, _, _ = position(dev_ref[0])
    outs = refs[2 * SIDE :]
    cols = outs[0].shape[2]
    rows = outs[0].shape[1]
    for g in range(GROUPS):
        at = slice(g * cols, (g + 1) * cols)
        for i in range(SIDE):
            outs[g][wrap(x + i)] = refs[i][:, :, at].reshape(rows, cols)
            outs[GROUPS + g][wrap(z + i)] = refs[SIDE + i][:, :, at].reshape(rows, cols)


def second_vo_kernel(dev_ref, *refs):
    z = position(dev_ref[0])[0]
    v_ref, o_ref = refs[SIDE:]
    half = v_ref.shape[3]
    rows = o_ref.shape[2]
    for i in range(SIDE):
        v_ref[wrap(z + i)] = refs[i][:, :, :half]
        o_ref[wrap(z + i), :, :, :half] = refs[i][:, :rows, half:]
        o_ref[wrap(z + i), :, :, half:] = refs[i][:, rows:, half:]


def merge(kernel, name, device, pieces, shapes):
    return pl.pallas_call(
        kernel,
        in_specs=[SMEM] + [VMEM] * len(pieces),
        out_specs=[VMEM] * len(shapes),
        out_shape=[jax.ShapeDtypeStruct(s, bf16) for s in shapes],
        compiler_params=pltpu.CompilerParams(vmem_limit_bytes=24 << 20),
        name=name,
    )(device, *pieces)


def attend_kernel(dev_ref, lens_ref, own_ref, other_ref, *refs, heads):
    q_refs, k_refs = refs[:SIDE], refs[SIDE : 2 * SIDE]
    g_ref, n_ref, w_ref, qk_ref, col_ref, n_sem, w_sem = refs[2 * SIDE :]
    slots = n_ref.shape[1]
    texts = own_ref.shape[0]
    step = pl.program_id(0)
    slot = lax.rem(step, 2)
    length = lens_ref[step]
    blocks = (length + 127) // 128
    pairs = heads // 2
    cols = heads * HEAD

    def fetch(text, place):
        @pl.when(text < texts)
        def _():
            pltpu.make_async_copy(own_ref.at[text], n_ref.at[place], n_sem.at[place]).start()

        @pl.when((text >= texts) & (text < 2 * texts))
        def _():
            pltpu.make_async_copy(
                other_ref.at[text - texts], n_ref.at[place], n_sem.at[place]
            ).start()

    @pl.when(step == 0)
    def _():
        z, x, _, _ = position(dev_ref[0])
        plane = q_refs[0].shape[0] * q_refs[0].shape[1]
        line = q_refs[0].shape[1]
        for i in range(SIDE):
            for j in range(SIDE):
                at = wrap(z + i) * plane + j * line
                pltpu.make_async_copy(
                    q_refs[i].at[j],
                    w_ref.at[pl.ds(pl.multiple_of(at, line), line), :cols],
                    w_sem,
                ).start()
                at = j * plane + wrap(x + i) * line
                pltpu.make_async_copy(
                    k_refs[i].at[j],
                    w_ref.at[pl.ds(pl.multiple_of(at, line), line), cols:],
                    w_sem,
                ).start()
        fetch(step, slot)
        pltpu.make_async_copy(w_ref, w_ref, w_sem).wait()

    pltpu.make_async_copy(own_ref.at[0], n_ref.at[slot], n_sem.at[slot]).wait()
    fetch(step + 1, 1 - slot)

    def run(size):
        rows = n_ref[slot, :size, :]
        for tile in range(heads // 2):
            out = jnp.dot(
                rows, w_ref[:, tile * 256 : (tile + 1) * 256], preferred_element_type=f32
            ).astype(bf16)
            qk_ref[2 * tile, :size, :] = out[:, :128]
            qk_ref[2 * tile + 1, :size, :] = out[:, 128:]
        col_ref[...] = jnp.zeros_like(col_ref)
        tail = size - 128
        key_id = tail + lax.broadcasted_iota(jnp.int32, (128, 1), 0)

        def pair(p, carry):
            keys = qk_ref[pairs + p, :size, :]
            lane = lax.broadcasted_iota(jnp.int32, (size, 128), 1)
            for half in range(2):
                key_half = jnp.where((lane < HEAD) == (half == 0), keys, jnp.zeros_like(keys))
                acc = jnp.zeros((size, 128), f32)
                for start in range(0, size, 128):
                    query = qk_ref[p, start : start + 128, :]
                    s = lax.dot_general(
                        key_half, query, (((1,), (1,)), ((), ())), preferred_element_type=f32
                    )
                    last = jnp.where(key_id < length, s[tail:, :], NEG)
                    s = jnp.concatenate([s[:tail, :], last], axis=0) if tail else last
                    e = jnp.exp(s - jnp.max(s, axis=0, keepdims=True))
                    total = jnp.sum(e, axis=0, keepdims=True)
                    query_id = start + lax.broadcasted_iota(jnp.int32, (1, 128), 1)
                    acc = acc + e * jnp.where(query_id < length, 1.0 / total, 0.0)
                column = jnp.sum(acc, axis=1, keepdims=True)
                col_ref[:size, :] = jnp.where(lane == 2 * p + half, column, col_ref[:size, :])
            return carry

        lax.fori_loop(0, pairs, pair, 0)
        hi, lo = split(col_ref[:size, :])
        dims = (((0,), (0,)), ((), ()))
        g = lax.dot_general(hi, rows, dims, preferred_element_type=f32)
        g = g + lax.dot_general(lo, rows, dims, preferred_element_type=f32)
        g_ref[0] = g[:heads, :]

    for b in range(1, slots // 128 + 1):
        pl.when(blocks == b)(functools.partial(run, 128 * b))


def attend(device, lens, own, other, q_pieces, k_pieces):
    texts, slots, width = own.shape
    cols = q_pieces[0].shape[2]
    heads = cols // HEAD
    return pl.pallas_call(
        functools.partial(attend_kernel, heads=heads),
        grid=(2 * texts,),
        in_specs=[SMEM, SMEM] + [ANY] * (2 + 2 * SIDE),
        out_specs=pl.BlockSpec((1, heads, width), lambda t: (t, 0, 0)),
        scratch_shapes=[
            pltpu.VMEM((2, slots, width), bf16),
            pltpu.VMEM((width, 2 * cols), bf16),
            pltpu.VMEM((heads, slots, 128), bf16),
            pltpu.VMEM((slots, 128), f32),
            pltpu.SemaphoreType.DMA((2,)),
            pltpu.SemaphoreType.DMA,
        ],
        out_shape=jax.ShapeDtypeStruct((2 * texts, heads, width), f32),
        compiler_params=pltpu.CompilerParams(vmem_limit_bytes=40 << 20),
        cost_estimate=pl.CostEstimate(
            flops=8 * texts * slots * width * cols,
            bytes_accessed=4 * texts * slots * width + 4 * width * cols,
            transcendentals=2 * texts * heads * slots * slots,
        ),
        name="attend",
    )(device, lens, own, other, *q_pieces, *k_pieces)


def context_kernel(dev_ref, *refs, texts, heads):
    g_refs, v_refs = refs[:GROUPS], refs[GROUPS : GROUPS + SIDE]
    out_ref, w_ref, sem = refs[GROUPS + SIDE :]
    y = position(dev_ref[0])[2]
    lines, rows = v_refs[0].shape[:2]
    for i in range(SIDE):
        for j in range(lines):
            at = pl.multiple_of(j * rows * SIDE + wrap(y + i) * rows, rows)
            pltpu.make_async_copy(v_refs[i].at[j], w_ref.at[pl.ds(at, rows), :], sem).start()
    width = w_ref.shape[0]
    per = heads // GROUPS
    g = jnp.concatenate([r[...].reshape(texts * per, width) for r in g_refs], axis=0)
    lhs = jnp.concatenate(split(g), axis=0)
    pltpu.make_async_copy(w_ref, w_ref, sem).wait()
    both = jnp.dot(lhs, w_ref[...], preferred_element_type=f32)
    both = both[: texts * heads] + both[texts * heads :]
    own = jnp.zeros((texts, heads * HEAD), f32)
    for n in range(GROUPS):
        part = both[n * texts * per : (n + 1) * texts * per].reshape(texts, per, heads * HEAD)
        head = n * per + lax.broadcasted_iota(jnp.int32, part.shape, 1)
        lane = lax.broadcasted_iota(jnp.int32, part.shape, 2)
        own = own + jnp.sum(jnp.where(lane // HEAD == head, part, 0.0), axis=1)
    out_ref[...] = jnp.concatenate([own, jnp.zeros_like(own)], axis=0)


def context_of(device, gs, v_pieces, heads):
    texts, _, width = gs[0].shape
    return pl.pallas_call(
        functools.partial(context_kernel, texts=texts, heads=heads),
        in_specs=[SMEM] + [VMEM] * GROUPS + [ANY] * SIDE,
        out_specs=VMEM,
        scratch_shapes=[pltpu.VMEM((width, heads * HEAD), bf16), pltpu.SemaphoreType.DMA],
        out_shape=jax.ShapeDtypeStruct((2 * texts, heads * HEAD), f32),
        compiler_params=pltpu.CompilerParams(vmem_limit_bytes=24 << 20),
        name="context",
    )(device, *gs, *v_pieces)


def unit_kernel(dev_ref, mine_ref, theirs_ref, sum_ref, len_ref, ord_ref, *refs):
    near_refs, far_refs = refs[:SIDE], refs[SIDE : 2 * SIDE]
    out_ref, wa_ref, wb_ref, sem_a, sem_b = refs[2 * SIDE :]
    _, _, y, core = position(dev_ref[0])
    lines, rows = near_refs[0].shape[:2]
    for pieces, w_ref, sem in ((near_refs, wa_ref, sem_a), (far_refs, wb_ref, sem_b)):
        for i in range(SIDE):
            for j in range(lines):
                at = pl.multiple_of(j * rows * SIDE + wrap(y + i) * rows, rows)
                pltpu.make_async_copy(pieces[i].at[j], w_ref.at[pl.ds(at, rows), :], sem).start()
    half = mine_ref.shape[1]
    width = sum_ref.shape[1]
    cols = wa_ref.shape[1]
    mine = jnp.concatenate(split(mine_ref[...]), axis=0)
    theirs = jnp.concatenate(split(theirs_ref[...]), axis=0)
    tall = mine_ref.shape[0]

    def project(w_ref):
        top = w_ref[pl.ds(pl.multiple_of(core * half, half), half), :]
        bottom = w_ref[pl.ds(pl.multiple_of((1 - core) * half, half), half), :]
        a = jnp.dot(mine, top, preferred_element_type=f32)
        b = jnp.dot(theirs, bottom, preferred_element_type=f32)
        return (a[0:2] + a[tall : tall + 2]) + (b[2:4] + b[tall + 2 : tall + 4])

    near = pl.ds(pl.multiple_of(core * cols, cols), cols)
    far = pl.ds(pl.multiple_of((1 - core) * cols, cols), cols)
    inv = 1.0 / len_ref[...]
    pltpu.make_async_copy(wa_ref, wa_ref, sem_a).wait()
    pa = (sum_ref[:, near] + project(wa_ref)) * inv
    pltpu.make_async_copy(wb_ref, wb_ref, sem_b).wait()
    pb = (sum_ref[:, far] + project(wb_ref)) * inv
    square = jnp.sum(pa * pa, axis=1, keepdims=True) + jnp.sum(pb * pb, axis=1, keepdims=True)
    scale = lax.rsqrt(square * (1.0 / width) + 1e-06)
    out_ref[:, near] = (pa * scale).astype(bf16)
    out_ref[:, far] = (pb * scale).astype(bf16)
    out_ref[:, width:] = jnp.broadcast_to(ord_ref[...], (2, 128)).astype(bf16)


def unit_of(device, mine, theirs, total, lens, order, near, far):
    texts, width = total.shape
    features = 2 * mine.shape[1]
    return pl.pallas_call(
        unit_kernel,
        in_specs=[SMEM] + [VMEM] * 5 + [ANY] * (2 * SIDE),
        out_specs=VMEM,
        scratch_shapes=[pltpu.VMEM((features, width // 2), bf16)] * 2
        + [pltpu.SemaphoreType.DMA] * 2,
        out_shape=jax.ShapeDtypeStruct((texts, width + 128), bf16),
        compiler_params=pltpu.CompilerParams(vmem_limit_bytes=24 << 20),
        name="unit",
    )(device, mine, theirs, total, lens, order, *near, *far)


def score_kernel(dev_ref, ua_ref, ub_ref, rows_ref, cand_ref, out_ref):
    own, width = rows_ref.shape
    pairs = cand_ref.shape[0]
    near = cand_ref[...] - dev_ref[0] * own
    valid = (near >= 0) & (near < own)
    tile = near // 128
    within = jnp.where(valid, near - tile * 128, 0)
    lane = lax.broadcasted_iota(jnp.int32, near.shape, 1)
    picked = jnp.zeros(near.shape, f32)
    for odd in range(2):
        units = jnp.zeros((pairs, width), f32)
        for u_ref in (ua_ref, ub_ref):
            rank = u_ref[:, width:].astype(f32)
            place = 2 * lax.broadcasted_iota(jnp.int32, rank.shape, 1) + odd
            hot = (rank == place.astype(f32)).astype(bf16)
            units = units + lax.dot_general(
                hot, u_ref[:, :width], (((0,), (0,)), ((), ())), preferred_element_type=f32
            )
        local = lax.dot_general(
            units.astype(bf16), rows_ref[...], (((1,), (1,)), ((), ())), preferred_element_type=f32
        )
        side = valid & ((lane >= 64) == (odd == 1))
        for k in range(own // 128):
            got = jnp.take_along_axis(local[:, k * 128 : (k + 1) * 128], within, axis=1)
            picked = jnp.where(side & (tile == k), got, picked)
    out_ref[...] = picked


def scores_of(device, ua, ub, rows, cand):
    return pl.pallas_call(
        score_kernel,
        in_specs=[SMEM] + [VMEM] * 4,
        out_specs=VMEM,
        out_shape=jax.ShapeDtypeStruct(cand.shape, f32),
        compiler_params=pltpu.CompilerParams(vmem_limit_bytes=32 << 20),
        name="scores",
    )(device, ua, ub, rows, cand)


def per_device(
    devices, hidden, lengths, order, candidates, norm_gain, w_query, w_key, w_value, w_out, index_rows
):
    texts, slots, width = hidden.shape
    half = w_query.shape[1] // 2
    heads = half // HEAD
    index = lax.axis_index("dp")
    device = index.reshape(1)
    swap_pairs = [(d, d ^ 1) for d in range(devices)]
    same_core = [list(range(c, devices, 2)) for c in range(2)]

    def swap(x):
        return lax.ppermute(x, "dp", swap_pairs)

    def line(x, dim):
        unit = (32, 8, 2)[dim]
        pieces = [x]
        for i in range(1, SIDE):
            pairs = []
            for d in range(devices):
                at = position(d)[dim]
                pairs.append((d, d + ((at - i) % SIDE - at) * unit))
            pieces.append(lax.ppermute(x, "dp", pairs))
        return pieces

    Z, X, Y = 0, 1, 2
    raw = (w_query, w_key, w_value, w_out)
    rows = 2 * w_query.shape[0]
    qk, vo = merge(
        block_kernel,
        "block",
        device,
        raw + tuple(swap(w) for w in raw),
        [(rows, 2 * half)] * 2,
    )
    q, k = merge(first_qk_kernel, "first_qk", device, line(qk, Y), [(SIDE, rows, half)] * 2)
    (vo,) = merge(first_vo_kernel, "first_vo", device, line(vo, X), [(SIDE, rows, 2 * half)])
    groups = merge(
        second_qk_kernel,
        "second_qk",
        device,
        line(q, X) + line(k, Z),
        [(SIDE, SIDE * rows, half // GROUPS)] * (2 * GROUPS),
    )
    v, o = merge(
        second_vo_kernel,
        "second_vo",
        device,
        line(vo, Z),
        [(SIDE, SIDE, rows, half), (SIDE, SIDE, rows // 2, 2 * half)],
    )

    values = hidden.astype(f32)
    meansq = jnp.mean(values * values, axis=-1, keepdims=True)
    normed = (values * lax.rsqrt(meansq + 1e-06) * norm_gain).astype(bf16)
    other = swap(normed)
    lens = jnp.concatenate([lengths, swap(lengths)])
    valid = jnp.arange(slots, dtype=jnp.int32)[None, :] < lengths[:, None]
    total = jnp.sum(jnp.where(valid[:, :, None], values, 0.0), axis=1)

    finals = [(line(groups[g], Z), line(groups[GROUPS + g], X)) for g in range(GROUPS)]
    v_pieces = line(v.reshape(SIDE * SIDE, rows, half), Y)
    near = line(o.reshape(SIDE * SIDE, rows // 2, 2 * half), Y)
    far = [swap(piece) for piece in near]
    gs = [attend(device, lens, normed, other, *finals[g]) for g in range(GROUPS)]
    mine = context_of(device, gs, v_pieces, heads)
    theirs = swap(mine)
    unit = unit_of(
        device,
        mine,
        theirs,
        total,
        lengths.astype(f32).reshape(texts, 1),
        order.astype(f32).reshape(texts, 1),
        near,
        far,
    )
    copies = jnp.broadcast_to(unit[None], (devices // 2,) + unit.shape)
    units = lax.all_to_all(copies, "dp", 0, 0, tiled=True, axis_index_groups=same_core)
    ua = units.reshape(devices, unit.shape[1])
    ub = swap(ua)
    cand = candidates.reshape(devices, 2 * candidates.shape[1])
    picked = scores_of(device, ua, ub, index_rows, cand)
    back = lax.all_to_all(picked.reshape(devices, 1, picked.shape[1]), "dp", 0, 0, tiled=True)
    return jnp.sum(back, axis=(0, 1)).reshape(texts, candidates.shape[1])


def solution(mesh):
    devices = mesh.shape["dp"]
    return jax.shard_map(
        functools.partial(per_device, devices),
        mesh=mesh,
        in_specs=(
            P("dp", None, None),
            P("dp"),
            P("dp"),
            P(),
            P(),
            P("dp", None),
            P("dp", None),
            P("dp", None),
            P("dp", None),
            P("dp", None),
        ),
        out_specs=P("dp", None),
        check_vma=False,
    )
```
